32 devices in a mesh: row: 16 (over z, x, core), col: 2 (over y).
Axes of the slice: x: 2, y: 2, z: 4, core: 2. Of those that a mesh axis runs over, the one named last changes fastest.
Arguments:
- template: float32 [32, 16, 2048], P(None, 'row', 'col'), may hold values from -6 to 6
- target: float32 [32, 16, 2048], P(None, 'row', 'col'), may hold values from -6 to 6
- velocity: float32 [3, 32, 16, 2048], P(None, None, 'row', 'col'), may hold values from -0.6 to 0.6
- departure: int32 [32, 1, 2048], P('row', None, 'col'), may hold values from -48 to 48
- weights: float32 [8, 4], replicated, may hold values from -0.1 to 1, as said below
Outputs:
- gradient: float32 [3, 32, 16, 2048], P(None, 'row', 'col')
The draws below stay inside these ranges and needn't reach their ends.
Inputs may be any that keep to these rules, and one draw needn't show every extreme that they name: Row q holds the four weights of a cubic interpolation at a fraction between q / 8 and (q + 1) / 8; each row sums to one.
All inputs are finite; a program needn't handle non-finite values.
Results may differ from the reference program's by a relative error of at most 0.0001.
Values sent between devices are 32-bit elements; how exact they have to be, the bound alone decides.
A program may use at most 64 MiB of HBM per device.

```python
import math
import jax
import jax.numpy as jnp

NZ = 2048
LB = 16
QUANT = 8
SHIFT = 6
TAPS = 4
NX = 32
NY = 16


def draw_weights(key, part):
    levels = jnp.arange(QUANT, dtype=jnp.float32)[:, None]
    spread = jax.random.uniform(key, (QUANT, 1), jnp.float32)
    point = (levels + spread) / QUANT
    tap_first = -point * (point - 1.0) * (point - 2.0) / 6.0
    tap_second = (point + 1.0) * (point - 1.0) * (point - 2.0) / 2.0
    tap_third = -(point + 1.0) * point * (point - 2.0) / 2.0
    tap_fourth = (point + 1.0) * point * (point - 1.0) / 6.0
    return jnp.concatenate([tap_first, tap_second, tap_third, tap_fourth], axis=1)


def with_ends(values, own_key, least, largest):
    dims = values.shape
    index_at = [jax.random.randint(jax.random.fold_in(own_key, axis), (), 0, dims[axis]) for axis in range(len(dims))]
    values = values.at[tuple(index_at)].set(least)
    longest = dims.index(max(dims))
    index_at[longest] = (index_at[longest] + 1) % dims[longest]
    return values.at[tuple(index_at)].set(largest)


def shard_levels(own_key, extent, pieces, low, largest):
    gain = 1.0
    for position, blocks in pieces:
        draws = jax.random.uniform(jax.random.fold_in(jax.random.fold_in(own_key, 6), position), (blocks,), jnp.float32, low / len(pieces), largest / len(pieces))
        gain = gain * jnp.repeat(jnp.exp(draws), extent[position] // blocks).reshape((-1,) + (1,) * (len(extent) - 1 - position))
    return gain


def normal_values(stream_key, dims, scale, most, pieces=(), kind=jnp.bfloat16):
    array = jax.random.normal(stream_key, dims, jnp.float32) * scale
    if len(pieces) > 0:
        array = shard_levels(stream_key, dims, pieces, -0.22, 0.18) * array
    return jnp.clip(array, min=-most, max=most).astype(kind)


def setup_inputs(seed: int = 0) -> dict:
    splits = jax.random.split(jax.random.key(seed), 6)
    template = normal_values(splits[0], (NX, NY, NZ), 1.0, 6.0, ((1, 16), (2, 2)), jnp.float32)
    target = normal_values(splits[1], (NX, NY, NZ), 1.0, 6.0, ((1, 16), (2, 2)), jnp.float32)
    velocity = normal_values(splits[2], (3, NX, NY, NZ), 0.1, 0.6, ((2, 16), (3, 2)), jnp.float32)
    departure = with_ends(jax.random.randint(splits[3], (NX, NY // LB, NZ), -SHIFT * QUANT, SHIFT * QUANT + 1), jax.random.fold_in(splits[3], 1), -SHIFT * QUANT, SHIFT * QUANT).astype(jnp.int32)
    weights = draw_weights(jax.random.fold_in(splits[5], 71), 0)
    return dict(template=template, target=target, velocity=velocity, departure=departure, weights=weights)


BETA = 0.5


def central(values, axis):
    return (jnp.roll(values, -1, axis) - jnp.roll(values, 1, axis)) * 0.5


def second_difference(values, axis):
    return 2.0 * values - jnp.roll(values, -1, axis) - jnp.roll(values, 1, axis)


def reference(template, target, velocity, departure, weights):
    shift_cells = jnp.floor_divide(departure, QUANT).astype(jnp.int32)
    levels = (departure - shift_cells * QUANT).astype(jnp.int32)
    shift_cells = jnp.repeat(shift_cells, LB, axis=1)
    levels = jnp.repeat(levels, LB, axis=1)
    lines = template.shape[1]
    line_index = jnp.arange(lines, dtype=jnp.int32)[None, :, None]
    moved_image = jnp.zeros(template.shape, jnp.float32)
    for tap in range(TAPS):
        source_index = jnp.mod(line_index - shift_cells - 1 + tap, lines).astype(jnp.int32)
        moved_image = moved_image + weights[levels, tap] * jnp.take_along_axis(template, source_index, axis=1)
    misfit = target - moved_image
    frequency = jnp.fft.fftfreq(NZ) * NZ
    symbol = ((2.0 * math.pi / NZ) * frequency) ** 2
    components = []
    for comp_index in range(3):
        component = velocity[comp_index]
        second = second_difference(component, 0) + second_difference(component, 1)
        spectrum = jnp.fft.fft(component, axis=2)
        bending = jnp.real(jnp.fft.ifft(spectrum * symbol, axis=2)).astype(jnp.float32)
        force = misfit * central(moved_image, comp_index)
        components.append(BETA * (second + bending) + force)
    return jnp.stack(components)
```

```python
import functools
import math

import jax
import jax.numpy as jnp
import numpy as np
from jax import lax
from jax.experimental import pallas as pl
from jax.experimental.pallas import tpu as pltpu
from jax.sharding import PartitionSpec as P

QUANT = 8
TAPS = 4


BETA = 0.5
HIGH = lax.Precision.HIGHEST
LANES = 128
SUBLANES = 8
MESH = pl.DeviceIdType.MESH


def with_halo(block, sides, width):
    for axis, dim in sides:
        count = lax.axis_size(axis)
        forward = [(i, i + 1) for i in range(count - 1)]
        forward.append((count - 1, 0))
        backward = [(target, source) for source, target in forward]
        low = lax.ppermute(
            lax.slice_in_dim(block, block.shape[dim] - width, None, axis=dim), axis, forward
        )
        high = lax.ppermute(lax.slice_in_dim(block, 0, width, axis=dim), axis, backward)
        block = jnp.concatenate([low, block, high], axis=dim)
    return block


def central(values, axis):
    return (jnp.roll(values, -1, axis) - jnp.roll(values, 1, axis)) * 0.5


def second_difference(values, axis):
    return 2.0 * values - jnp.roll(values, -1, axis) - jnp.roll(values, 1, axis)


def tap_weights(levels, weight):
    taps = []
    for tap in range(TAPS):
        value = jnp.zeros(levels.shape, jnp.float32)
        for level in range(QUANT):
            value = jnp.where(levels == level, weight(level, tap), value)
        taps.append(value)
    return taps


def transport(template_y, departure, weights):
    planes, lines, columns = template_y.shape
    blocks = departure.shape[1]
    span = lines // blocks
    shift_cells = jnp.floor_divide(departure, QUANT)
    levels = departure - shift_cells * QUANT
    taps = tap_weights(levels, lambda level, tap: weights[level, tap])
    shift = jnp.mod(shift_cells + 1, lines)
    parts = []
    for block in range(blocks):
        rolled = template_y
        step = 1
        while step < lines:
            chosen = (shift[:, block : block + 1] & step) != 0
            rolled = jnp.where(chosen, jnp.roll(rolled, step, 1), rolled)
            step *= 2
        part = 0.0
        for tap in range(TAPS):
            turned = jnp.roll(rolled, -tap - block * span, 1)[:, :span]
            part = part + taps[tap][:, block : block + 1] * turned
        parts.append(part)
    return jnp.concatenate(parts, axis=1)


def curvature(velocity_z):
    field_shape = velocity_z.shape
    length = field_shape[-1]
    inner = 128
    outer = length // inner
    lines = velocity_z.reshape(-1, outer, inner)
    angle = 2.0 * math.pi / length
    outer_index = jnp.arange(outer, dtype=jnp.int32)
    inner_index = jnp.arange(inner, dtype=jnp.int32)
    outer_phase = (
        jnp.mod(outer_index[:, None] * outer_index[None, :] * inner, length).astype(jnp.float32)
        * angle
    )
    cos_outer = jnp.cos(outer_phase)
    sin_outer = jnp.sin(outer_phase)
    twist_phase = (
        jnp.mod(outer_index[:, None] * inner_index[None, :], length).astype(jnp.float32) * angle
    )
    cos_twist = jnp.cos(twist_phase)
    sin_twist = jnp.sin(twist_phase)
    inner_phase = (
        jnp.mod(inner_index[:, None] * inner_index[None, :] * outer, length).astype(jnp.float32)
        * angle
    )
    cos_inner = jnp.cos(inner_phase)
    sin_inner = jnp.sin(inner_phase)
    freq_index = outer_index[:, None] + outer * inner_index[None, :]
    signed = jnp.where(freq_index < length // 2, freq_index, freq_index - length).astype(
        jnp.float32
    )
    symbol = (signed * angle) ** 2 / length
    real_one = jnp.einsum("lap,ak->lkp", lines, cos_outer, precision=HIGH)
    imag_one = -jnp.einsum("lap,ak->lkp", lines, sin_outer, precision=HIGH)
    real_two = real_one * cos_twist + imag_one * sin_twist
    imag_two = imag_one * cos_twist - real_one * sin_twist
    real_three = jnp.einsum("lkp,pq->lkq", real_two, cos_inner, precision=HIGH) + jnp.einsum(
        "lkp,pq->lkq", imag_two, sin_inner, precision=HIGH
    )
    imag_three = jnp.einsum("lkp,pq->lkq", imag_two, cos_inner, precision=HIGH) - jnp.einsum(
        "lkp,pq->lkq", real_two, sin_inner, precision=HIGH
    )
    real_three = real_three * symbol
    imag_three = imag_three * symbol
    real_four = jnp.einsum("lkq,pq->lkp", real_three, cos_inner, precision=HIGH) - jnp.einsum(
        "lkq,pq->lkp", imag_three, sin_inner, precision=HIGH
    )
    imag_four = jnp.einsum("lkq,pq->lkp", imag_three, cos_inner, precision=HIGH) + jnp.einsum(
        "lkq,pq->lkp", real_three, sin_inner, precision=HIGH
    )
    real_five = real_four * cos_twist - imag_four * sin_twist
    imag_five = imag_four * cos_twist + real_four * sin_twist
    result = jnp.einsum("lkp,kn->lnp", real_five, cos_outer, precision=HIGH) - jnp.einsum(
        "lkp,kn->lnp", imag_five, sin_outer, precision=HIGH
    )
    return result.reshape(field_shape)


def spectral(arrived):
    return (arrived, curvature(arrived[3:6]))


def per_device(template, target, velocity, departure, weights):
    across = second_difference(velocity, 1)
    bundle = jnp.concatenate([template[None], target[None], velocity, across], axis=0)
    regrouped = lax.all_to_all(bundle, "row", split_axis=1, concat_axis=2, tiled=True)
    moved_image = transport(regrouped[0], departure, weights)
    misfit = regrouped[1] - moved_image
    pull_along = misfit * central(moved_image, 1)
    velocity_y = regrouped[2:5]
    second_part = second_difference(velocity_y, 2)
    second_part = regrouped[5:8] + second_part
    outgoing = jnp.concatenate(
        [misfit[None], moved_image[None], pull_along[None], velocity_y, second_part], axis=0
    )
    columns_z, bending = spectral(
        lax.all_to_all(outgoing, "col", split_axis=2, concat_axis=3, tiled=True)
    )
    misfit_z = columns_z[0]
    moved_z = columns_z[1]
    second_z = columns_z[6:9]
    padded = with_halo(moved_z, (("row", 0),), 1)
    slope_across = (padded[2:] - padded[:-2]) * 0.5
    force = jnp.stack([misfit_z * slope_across, columns_z[2], misfit_z * central(moved_z, 2)])
    return BETA * (second_z + bending) + force


def split_halves(values):
    high = values.astype(jnp.bfloat16)
    return high, (values - high.astype(jnp.float32)).astype(jnp.bfloat16)


def dot_split(left, right):
    dot = functools.partial(jnp.dot, preferred_element_type=jnp.float32)
    return dot(left[0], right[0]) + (dot(left[0], right[1]) + dot(left[1], right[0]))


def halves_of(matrix):
    high = matrix.astype(np.float32).astype(jnp.bfloat16)
    low = (matrix - high.astype(np.float64)).astype(np.float32).astype(jnp.bfloat16)
    return np.stack([high, low])


def operators(length, rows):
    outer = length // LANES
    frequency = np.fft.fftfreq(length) * length
    response = np.real(np.fft.ifft((2.0 * math.pi / length * frequency) ** 2))
    response[0] += 4.0
    response *= BETA
    inner = np.arange(LANES)
    group = np.arange(outer)
    away = np.mod(
        LANES * group[:, None, None] + inner[None, :, None] - inner[None, None, :], length
    )
    mixed = np.fft.fft(response[away], axis=0)
    pairs = []
    forward = np.zeros((outer, outer))
    inverse = np.zeros((outer, outer))
    forward[0] = 1.0
    forward[1] = (-1.0) ** group
    inverse[:, 0] = 1.0 / outer
    inverse[:, 1] = (-1.0) ** group / outer
    zero = np.zeros((LANES, LANES))
    pairs.append(np.block([[mixed[0].real.T, zero], [zero, mixed[outer // 2].real.T]]))
    for k in range(1, outer // 2):
        real, imag = mixed[k].real.T, mixed[k].imag.T
        pairs.append(np.block([[real, imag], [-imag, real]]))
        phase = 2.0 * math.pi * k * group / outer
        forward[2 * k] = np.cos(phase)
        forward[2 * k + 1] = -np.sin(phase)
        inverse[:, 2 * k] = 2.0 * np.cos(phase) / outer
        inverse[:, 2 * k + 1] = -2.0 * np.sin(phase) / outer
    same = np.eye(rows)
    ahead = np.einsum("ka,yz->kyza", forward, same).reshape(outer * rows, rows * outer)
    back = np.einsum("ak,yz->yakz", inverse, same).reshape(rows * outer, outer * rows)
    return halves_of(ahead), halves_of(np.stack(pairs)), halves_of(back)


def kernel(
    extent,
    template,
    target,
    velocity,
    departure,
    weights,
    ahead_hbm,
    pairs_hbm,
    back_hbm,
    out,
    template_y,
    target_z,
    velocity_z,
    extended,
    moved,
    moved_low,
    moved_high,
    velocity_low,
    velocity_high,
    spectrum,
    ahead,
    pairs,
    back,
    load_sem,
    send_sem,
    recv_sem,
):
    rows, columns = extent
    row, column = lax.axis_index("row"), lax.axis_index("col")
    planes, lines, slab = template_y.shape[:3]
    components = velocity_z.shape[0]
    own = lines // columns
    outer = columns * slab
    owner = row // own
    place = lax.rem(row, own)
    TEMPLATE, TARGET, MOVED, LOW, HIGH_SIDE, VELOCITY = 0, 1, 2, 3, 4, 5
    VLOW, VHIGH = VELOCITY + components, VELOCITY + 2 * components

    loads = [
        pltpu.make_async_copy(source, sink, load_sem.at[i])
        for i, (source, sink) in enumerate(
            [(ahead_hbm, ahead), (pairs_hbm, pairs), (back_hbm, back)]
        )
    ]
    for load in loads:
        load.start()

    barrier = pltpu.get_barrier_semaphore()
    for i in range(rows):
        for j in range(columns):
            if i + j > 0:
                pl.semaphore_signal(
                    barrier,
                    inc=1,
                    device_id=(lax.rem(row + i, rows), lax.rem(column + j, columns)),
                    device_id_type=MESH,
                )
    pl.semaphore_wait(barrier, rows * columns - 1)

    def remote(source, sink, kind, to):
        return pltpu.make_async_remote_copy(
            src_ref=source,
            dst_ref=sink,
            send_sem=send_sem.at[kind],
            recv_sem=recv_sem.at[kind],
            device_id=to,
            device_id_type=MESH,
        )

    pending = []

    def deliver(source, sink, kind, to, near):
        if near is None:
            remote(source, sink, kind, to).start()
            pending.append((None, source, sink, kind, to))
            return

        @pl.when(near == column)
        def _():
            pltpu.make_async_copy(source, sink, recv_sem.at[kind]).start()

        @pl.when(near != column)
        def _():
            remote(source, sink, kind, to).start()

        pending.append((near, source, sink, kind, to))

    def exchange(order):
        return [(i, lax.rem(row + i, rows)) for i in order]

    def arrived(ref, kind):
        pltpu.make_async_copy(ref, ref, recv_sem.at[kind]).wait()

    order = list(range(1, rows)) + [0]
    for i, to in exchange(order):
        source = template.at[pl.ds(to * planes, planes)]
        sink = template_y.at[:, row]
        if i == 0:
            pltpu.make_async_copy(source, sink, recv_sem.at[TEMPLATE]).start()
        else:
            deliver(source, sink, TEMPLATE, (to, column), None)
    for i, to in exchange(order):
        deliver(
            target.at[pl.ds(to * planes, planes)],
            target_z.at[:, place, column],
            TARGET,
            (to, owner),
            owner if i == 0 else None,
        )
    before = lax.rem(owner + columns - 1, columns)
    after = lax.rem(owner + 1, columns)

    def send_velocity(comp):
        for i, to in exchange(order):
            source = velocity.at[comp, pl.ds(to * planes, planes)]
            deliver(
                source,
                velocity_z.at[comp, :, place + 1, column],
                VELOCITY + comp,
                (to, owner),
                owner if i == 0 else None,
            )

    def edges(act):
        @pl.when(place == 0)
        def _():
            for comp in range(components):
                for i, to in exchange(order):
                    act(comp, i, to, own + 1, before)

        @pl.when(place == own - 1)
        def _():
            for comp in range(components):
                for i, to in exchange(order):
                    act(comp, i, to, 0, after)

    def edge_copy(comp, to, line, where):
        return (
            velocity.at[comp, pl.ds(to * planes, planes)],
            velocity_z.at[comp, :, line, column],
            VELOCITY + comp,
            (to, where),
        )

    def start_edge(comp, i, to, line, where):
        copy = edge_copy(comp, to, line, where)
        if i > 0:
            remote(*copy).start()
            return

        @pl.when(where == column)
        def _():
            pltpu.make_async_copy(copy[0], copy[1], recv_sem.at[copy[2]]).start()

        @pl.when(where != column)
        def _():
            remote(*copy).start()

    def wait_edge(comp, i, to, line, where):
        copy = edge_copy(comp, to, line, where)
        if i > 0:
            remote(*copy).wait_send()
            return

        @pl.when(where != column)
        def _():
            remote(*copy).wait_send()

    edges(start_edge)
    for comp in range(components):
        send_velocity(comp)

    arrived(template_y, TEMPLATE)
    blocks = departure.shape[1]
    span = lines // blocks
    for plane in range(planes):
        image = [template_y[plane, y] for y in range(lines)]
        for block in range(blocks):
            offset = departure[plane, block]
            whole = offset >> (QUANT.bit_length() - 1)
            levels = offset - whole * QUANT
            taps = tap_weights(levels, lambda level, tap: weights[level, tap])
            shift = jnp.where(whole + 1 < 0, whole + 1 + lines, whole + 1)
            rolled = image
            step = 1
            while step < lines:
                chosen = (shift & step) != 0
                rolled = [
                    jnp.where(chosen, rolled[(y - step) % lines], rolled[y]) for y in range(lines)
                ]
                step *= 2
            for y in range(block * span, (block + 1) * span):
                value = taps[0] * rolled[y]
                for tap in range(1, TAPS):
                    value = value + taps[tap] * rolled[(y + tap) % lines]
                extended[plane, y + 1] = value
                if y == lines - 1:
                    extended[plane, 0] = value
                if y == 0:
                    extended[plane, lines + 1] = value
    up, down = lax.rem(row + 1, rows), lax.rem(row + rows - 1, rows)
    for j in range(1, columns):
        to = lax.rem(column + j, columns)
        deliver(
            extended.at[:, pl.ds(to * own, own + 2)],
            moved.at[column],
            MOVED,
            (row, to),
            None,
        )
    for j in range(columns):
        to = lax.rem(column + j, columns)
        lines_of = pl.ds(to * own + 1, own)
        deliver(
            extended.at[planes - 1, lines_of], moved_low.at[:, column], LOW, (up, to), None
        )
        deliver(extended.at[0, lines_of], moved_high.at[:, column], HIGH_SIDE, (down, to), None)
    moved[column] = extended[:, pl.ds(column * own, own + 2)]
    for load in loads:
        load.wait()

    def whole_lines(values):
        return values.reshape(values.shape[:-3] + (outer, LANES))

    ahead_parts = (ahead[0], ahead[1])
    back_parts = (back[0], back[1])
    for comp in range(components):
        arrived(velocity_z.at[comp], VELOCITY + comp)
        deliver(
            velocity_z.at[comp, planes - 1, pl.ds(1, own)],
            velocity_low.at[comp],
            VLOW + comp,
            (up, column),
            None,
        )
        deliver(
            velocity_z.at[comp, 0, pl.ds(1, own)],
            velocity_high.at[comp],
            VHIGH + comp,
            (down, column),
            None,
        )
        for plane in range(planes):
            block = velocity_z[comp, plane, 1 : own + 1].reshape(own * outer, LANES)
            spectrum[:, comp, plane] = dot_split(ahead_parts, split_halves(block)).reshape(
                outer, own, LANES
            )
        if comp > 0:
            continue
        arrived(target_z, TARGET)
        for _ in range(columns - 1):
            pltpu.make_async_copy(moved.at[0], moved.at[0], recv_sem.at[MOVED]).wait()
        arrived(moved_low, LOW)
        arrived(moved_high, HIGH_SIDE)
        lane = lax.broadcasted_iota(jnp.int32, (own, outer, LANES), 2)
        for plane in range(planes):
            with_ends = jnp.concatenate(
                [moved[j, plane] for j in range(columns)], axis=1
            )
            here = with_ends[1 : own + 1]
            misfit = whole_lines(target_z[plane]) - here
            half = 0.5 * misfit

            def at(index):
                if index < 0:
                    return whole_lines(moved_low[...])
                if index == planes:
                    return whole_lines(moved_high[...])
                return jnp.concatenate(
                    [moved[j, index, 1 : own + 1] for j in range(columns)], axis=1
                )

            out[0, plane] = half * (at(plane + 1) - at(plane - 1))
            out[1, plane] = half * (with_ends[2:] - with_ends[:-2])
            following = jnp.roll(here, -1, 2)
            following = jnp.where(lane == LANES - 1, jnp.roll(following, -1, 1), following)
            previous = jnp.roll(here, 1, 2)
            previous = jnp.where(lane == 0, jnp.roll(previous, 1, 1), previous)
            out[2, plane] = half * (following - previous)

    for pair in range(outer // 2):
        shape = (components * planes * own, LANES)
        joined = jnp.concatenate(
            [spectrum[2 * pair].reshape(shape), spectrum[2 * pair + 1].reshape(shape)], axis=1
        )
        result = dot_split(split_halves(joined), (pairs[0, pair], pairs[1, pair]))
        shape = (components, planes, own, LANES)
        spectrum[2 * pair] = result[:, :LANES].reshape(shape)
        spectrum[2 * pair + 1] = result[:, LANES:].reshape(shape)

    for comp in range(components):
        arrived(velocity_low.at[comp], VLOW + comp)
        arrived(velocity_high.at[comp], VHIGH + comp)
        for plane in range(planes):
            block = spectrum[:, comp, plane].reshape(outer * own, LANES)
            smooth = dot_split(back_parts, split_halves(block)).reshape(own, outer, LANES)
            low = velocity_low[comp] if plane == 0 else velocity_z[comp, plane - 1, 1 : own + 1]
            high = (
                velocity_high[comp]
                if plane == planes - 1
                else velocity_z[comp, plane + 1, 1 : own + 1]
            )
            sides = whole_lines(
                (low + high) + (velocity_z[comp, plane, :own] + velocity_z[comp, plane, 2:])
            )
            out[comp, plane] = out[comp, plane] + (smooth - BETA * sides)

    for near, source, sink, kind, to in pending:
        if near is None:
            remote(source, sink, kind, to).wait_send()
        else:

            @pl.when(near != column)
            def _():
                remote(source, sink, kind, to).wait_send()

    edges(wait_edge)


def direct(template, target, velocity, departure, weights):
    rows, columns = lax.axis_size("row"), lax.axis_size("col")
    extent_x, _, cells = template.shape
    components = velocity.shape[0]
    planes = extent_x // rows
    lines = rows
    own = lines // columns
    slab = cells // LANES
    outer = slab * columns
    ahead, pairs, back = operators(cells * columns, own)
    tile = (slab, LANES)
    hbm = pl.BlockSpec(memory_space=pl.ANY)
    vmem = pl.BlockSpec(memory_space=pltpu.VMEM)
    smem = pl.BlockSpec(memory_space=pltpu.SMEM)
    kinds = 5 + 3 * components
    result = pl.pallas_call(
        functools.partial(kernel, (rows, columns)),
        out_shape=jax.ShapeDtypeStruct((components, planes, own, outer, LANES), jnp.float32),
        in_specs=[hbm, hbm, hbm, vmem, smem, hbm, hbm, hbm],
        out_specs=vmem,
        scratch_shapes=[
            pltpu.VMEM((planes, lines) + tile, jnp.float32),
            pltpu.VMEM((planes, own, columns) + tile, jnp.float32),
            pltpu.VMEM((components, planes, own + 2, columns) + tile, jnp.float32),
            pltpu.VMEM((planes, lines + 2) + tile, jnp.float32),
            pltpu.VMEM((columns, planes, own + 2) + tile, jnp.float32),
            pltpu.VMEM((own, columns) + tile, jnp.float32),
            pltpu.VMEM((own, columns) + tile, jnp.float32),
            pltpu.VMEM((components, own, columns) + tile, jnp.float32),
            pltpu.VMEM((components, own, columns) + tile, jnp.float32),
            pltpu.VMEM((outer, components, planes, own, LANES), jnp.float32),
            pltpu.VMEM(ahead.shape, jnp.bfloat16),
            pltpu.VMEM(pairs.shape, jnp.bfloat16),
            pltpu.VMEM(back.shape, jnp.bfloat16),
            pltpu.SemaphoreType.DMA((3,)),
            pltpu.SemaphoreType.DMA((kinds,)),
            pltpu.SemaphoreType.DMA((kinds,)),
        ],
        compiler_params=pltpu.CompilerParams(collective_id=0, has_side_effects=True),
    )(
        template.reshape((extent_x,) + tile),
        target.reshape((extent_x,) + tile),
        velocity.reshape((components, extent_x) + tile),
        departure.reshape(departure.shape[:2] + tile),
        weights,
        jnp.asarray(ahead),
        jnp.asarray(pairs),
        jnp.asarray(back),
    )
    return result.reshape(components, planes, own, outer * LANES)


def per_block(template, target, velocity, departure, weights):
    rows, columns = lax.axis_size("row"), lax.axis_size("col")
    one_line = template.shape[1] == 1 and rows % columns == 0 and rows > 2
    whole_tiles = template.shape[2] % (LANES * SUBLANES) == 0
    short = rows // columns % SUBLANES == 0 and rows >= 8
    if one_line and whole_tiles and short:
        return direct(template, target, velocity, departure, weights)
    return per_device(template, target, velocity, departure, weights)


def solution(mesh):
    in_specs = (
        P(None, "row", "col"),
        P(None, "row", "col"),
        P(None, None, "row", "col"),
        P("row", None, "col"),
        P(),
    )
    out_specs = P(None, "row", "col", None)
    return jax.shard_map(
        per_block, mesh=mesh, in_specs=in_specs, out_specs=out_specs, check_vma=False
    )
```

```python
import functools
import math

import jax
import jax.numpy as jnp
import numpy as np
from jax import lax
from jax.experimental import pallas as pl
from jax.experimental.pallas import tpu as pltpu
from jax.sharding import PartitionSpec as P

QUANT = 8
TAPS = 4


BETA = 0.5
HIGH = lax.Precision.HIGHEST
LANES = 128
SUBLANES = 8
MESH = pl.DeviceIdType.MESH


def with_halo(block, sides, width):
    for axis, dim in sides:
        count = lax.axis_size(axis)
        forward = [(i, i + 1) for i in range(count - 1)]
        forward.append((count - 1, 0))
        backward = [(target, source) for source, target in forward]
        low = lax.ppermute(
            lax.slice_in_dim(block, block.shape[dim] - width, None, axis=dim), axis, forward
        )
        high = lax.ppermute(lax.slice_in_dim(block, 0, width, axis=dim), axis, backward)
        block = jnp.concatenate([low, block, high], axis=dim)
    return block


def central(values, axis):
    return (jnp.roll(values, -1, axis) - jnp.roll(values, 1, axis)) * 0.5


def second_difference(values, axis):
    return 2.0 * values - jnp.roll(values, -1, axis) - jnp.roll(values, 1, axis)


def tap_weights(levels, weight):
    taps = []
    for tap in range(TAPS):
        value = jnp.zeros(levels.shape, jnp.float32)
        for level in range(QUANT):
            value = jnp.where(levels == level, weight(level, tap), value)
        taps.append(value)
    return taps


def transport(template_y, departure, weights):
    planes, lines, columns = template_y.shape
    blocks = departure.shape[1]
    span = lines // blocks
    shift_cells = jnp.floor_divide(departure, QUANT)
    levels = departure - shift_cells * QUANT
    taps = tap_weights(levels, lambda level, tap: weights[level, tap])
    shift = jnp.mod(shift_cells + 1, lines)
    parts = []
    for block in range(blocks):
        rolled = template_y
        step = 1
        while step < lines:
            chosen = (shift[:, block : block + 1] & step) != 0
            rolled = jnp.where(chosen, jnp.roll(rolled, step, 1), rolled)
            step *= 2
        part = 0.0
        for tap in range(TAPS):
            turned = jnp.roll(rolled, -tap - block * span, 1)[:, :span]
            part = part + taps[tap][:, block : block + 1] * turned
        parts.append(part)
    return jnp.concatenate(parts, axis=1)


def curvature(velocity_z):
    field_shape = velocity_z.shape
    length = field_shape[-1]
    inner = 128
    outer = length // inner
    lines = velocity_z.reshape(-1, outer, inner)
    angle = 2.0 * math.pi / length
    outer_index = jnp.arange(outer, dtype=jnp.int32)
    inner_index = jnp.arange(inner, dtype=jnp.int32)
    outer_phase = (
        jnp.mod(outer_index[:, None] * outer_index[None, :] * inner, length).astype(jnp.float32)
        * angle
    )
    cos_outer = jnp.cos(outer_phase)
    sin_outer = jnp.sin(outer_phase)
    twist_phase = (
        jnp.mod(outer_index[:, None] * inner_index[None, :], length).astype(jnp.float32) * angle
    )
    cos_twist = jnp.cos(twist_phase)
    sin_twist = jnp.sin(twist_phase)
    inner_phase = (
        jnp.mod(inner_index[:, None] * inner_index[None, :] * outer, length).astype(jnp.float32)
        * angle
    )
    cos_inner = jnp.cos(inner_phase)
    sin_inner = jnp.sin(inner_phase)
    freq_index = outer_index[:, None] + outer * inner_index[None, :]
    signed = jnp.where(freq_index < length // 2, freq_index, freq_index - length).astype(
        jnp.float32
    )
    symbol = (signed * angle) ** 2 / length
    real_one = jnp.einsum("lap,ak->lkp", lines, cos_outer, precision=HIGH)
    imag_one = -jnp.einsum("lap,ak->lkp", lines, sin_outer, precision=HIGH)
    real_two = real_one * cos_twist + imag_one * sin_twist
    imag_two = imag_one * cos_twist - real_one * sin_twist
    real_three = jnp.einsum("lkp,pq->lkq", real_two, cos_inner, precision=HIGH) + jnp.einsum(
        "lkp,pq->lkq", imag_two, sin_inner, precision=HIGH
    )
    imag_three = jnp.einsum("lkp,pq->lkq", imag_two, cos_inner, precision=HIGH) - jnp.einsum(
        "lkp,pq->lkq", real_two, sin_inner, precision=HIGH
    )
    real_three = real_three * symbol
    imag_three = imag_three * symbol
    real_four = jnp.einsum("lkq,pq->lkp", real_three, cos_inner, precision=HIGH) - jnp.einsum(
        "lkq,pq->lkp", imag_three, sin_inner, precision=HIGH
    )
    imag_four = jnp.einsum("lkq,pq->lkp", imag_three, cos_inner, precision=HIGH) + jnp.einsum(
        "lkq,pq->lkp", real_three, sin_inner, precision=HIGH
    )
    real_five = real_four * cos_twist - imag_four * sin_twist
    imag_five = imag_four * cos_twist + real_four * sin_twist
    result = jnp.einsum("lkp,kn->lnp", real_five, cos_outer, precision=HIGH) - jnp.einsum(
        "lkp,kn->lnp", imag_five, sin_outer, precision=HIGH
    )
    return result.reshape(field_shape)


def spectral(arrived):
    return (arrived, curvature(arrived[3:6]))


def per_device(template, target, velocity, departure, weights):
    across = second_difference(velocity, 1)
    bundle = jnp.concatenate([template[None], target[None], velocity, across], axis=0)
    regrouped = lax.all_to_all(bundle, "row", split_axis=1, concat_axis=2, tiled=True)
    moved_image = transport(regrouped[0], departure, weights)
    misfit = regrouped[1] - moved_image
    pull_along = misfit * central(moved_image, 1)
    velocity_y = regrouped[2:5]
    second_part = second_difference(velocity_y, 2)
    second_part = regrouped[5:8] + second_part
    outgoing = jnp.concatenate(
        [misfit[None], moved_image[None], pull_along[None], velocity_y, second_part], axis=0
    )
    columns_z, bending = spectral(
        lax.all_to_all(outgoing, "col", split_axis=2, concat_axis=3, tiled=True)
    )
    misfit_z = columns_z[0]
    moved_z = columns_z[1]
    second_z = columns_z[6:9]
    padded = with_halo(moved_z, (("row", 0),), 1)
    slope_across = (padded[2:] - padded[:-2]) * 0.5
    force = jnp.stack([misfit_z * slope_across, columns_z[2], misfit_z * central(moved_z, 2)])
    return BETA * (second_z + bending) + force


def split_halves(values):
    high = values.astype(jnp.bfloat16)
    return high, (values - high.astype(jnp.float32)).astype(jnp.bfloat16)


def dot_split(left, right):
    dot = functools.partial(jnp.dot, preferred_element_type=jnp.float32)
    return dot(left[0], right[0]) + (dot(left[0], right[1]) + dot(left[1], right[0]))


def halves_of(matrix):
    high = matrix.astype(np.float32).astype(jnp.bfloat16)
    low = (matrix - high.astype(np.float64)).astype(np.float32).astype(jnp.bfloat16)
    return np.stack([high, low])


def operators(length, rows):
    outer = length // LANES
    frequency = np.fft.fftfreq(length) * length
    response = np.real(np.fft.ifft((2.0 * math.pi / length * frequency) ** 2))
    response[0] += 4.0
    response *= BETA
    inner = np.arange(LANES)
    group = np.arange(outer)
    away = np.mod(
        LANES * group[:, None, None] + inner[None, :, None] - inner[None, None, :], length
    )
    mixed = np.fft.fft(response[away], axis=0)
    pairs = []
    forward = np.zeros((outer, outer))
    inverse = np.zeros((outer, outer))
    forward[0] = 1.0
    forward[1] = (-1.0) ** group
    inverse[:, 0] = 1.0 / outer
    inverse[:, 1] = (-1.0) ** group / outer
    zero = np.zeros((LANES, LANES))
    pairs.append(np.block([[mixed[0].real.T, zero], [zero, mixed[outer // 2].real.T]]))
    for k in range(1, outer // 2):
        real, imag = mixed[k].real.T, mixed[k].imag.T
        pairs.append(np.block([[real, imag], [-imag, real]]))
        phase = 2.0 * math.pi * k * group / outer
        forward[2 * k] = np.cos(phase)
        forward[2 * k + 1] = -np.sin(phase)
        inverse[:, 2 * k] = 2.0 * np.cos(phase) / outer
        inverse[:, 2 * k + 1] = -2.0 * np.sin(phase) / outer
    same = np.eye(rows)
    ahead = np.einsum("ka,yz->kyza", forward, same).reshape(outer * rows, rows * outer)
    back = np.einsum("ak,yz->aykz", inverse, same).reshape(outer * rows, outer * rows)
    moves = np.einsum("ab,yz->ayzb", np.eye(outer), same).reshape(outer * rows, rows * outer)
    back = np.concatenate([back, moves], axis=1)
    return halves_of(ahead), halves_of(np.stack(pairs)), halves_of(back)


def kernel(
    extent,
    template,
    target,
    velocity,
    departure,
    weights,
    ahead_hbm,
    pairs_hbm,
    back_hbm,
    out,
    template_y,
    target_z,
    velocity_z,
    edge,
    extended,
    moved,
    moved_low,
    moved_high,
    rest,
    spectrum,
    ahead,
    pairs,
    back,
    load_sem,
    send_sem,
    recv_sem,
):
    rows, columns = extent
    row, column = lax.axis_index("row"), lax.axis_index("col")
    planes, lines, slab = template_y.shape[:3]
    components = velocity_z.shape[0]
    own = lines // columns
    outer = columns * slab
    owner = row // own
    place = lax.rem(row, own)
    TEMPLATE, TARGET, MOVED, LOW, HIGH_SIDE, VELOCITY = 0, 1, 2, 3, 4, 5
    SIDE, EDGE = VELOCITY + components, VELOCITY + 2 * components
    extent_x = velocity.shape[1]
    parity = lax.rem(row, 2)
    groups = [pl.ds(0, 1), pl.ds(1, components - 1)]

    loads = [
        pltpu.make_async_copy(source, sink, load_sem.at[i])
        for i, (source, sink) in enumerate(
            [(ahead_hbm, ahead), (pairs_hbm, pairs), (back_hbm, back)]
        )
    ]
    for load in loads:
        load.start()

    barrier = pltpu.get_barrier_semaphore()
    for i in range(rows):
        for j in range(columns):
            if i + j > 0:
                pl.semaphore_signal(
                    barrier,
                    inc=1,
                    device_id=(lax.rem(row + i, rows), lax.rem(column + j, columns)),
                    device_id_type=MESH,
                )
    pl.semaphore_wait(barrier, rows * columns - 1)

    def remote(source, sink, kind, to):
        return pltpu.make_async_remote_copy(
            src_ref=source,
            dst_ref=sink,
            send_sem=send_sem.at[kind],
            recv_sem=recv_sem.at[kind],
            device_id=to,
            device_id_type=MESH,
        )

    pending = []

    def deliver(source, sink, kind, to, near):
        if near is None:
            remote(source, sink, kind, to).start()
            pending.append((None, source, sink, kind, to))
            return

        @pl.when(near == column)
        def _():
            pltpu.make_async_copy(source, sink, recv_sem.at[kind]).start()

        @pl.when(near != column)
        def _():
            remote(source, sink, kind, to).start()

        pending.append((near, source, sink, kind, to))

    def exchange(order):
        return [(i, lax.rem(row + i, rows)) for i in order]

    def arrived(ref, kind):
        pltpu.make_async_copy(ref, ref, recv_sem.at[kind]).wait()

    order = sorted(range(rows), key=lambda i: abs(2 * i - rows))
    for i, to in exchange(order):
        source = template.at[pl.ds(to * planes, planes)]
        sink = template_y.at[:, row]
        if i == 0:
            pltpu.make_async_copy(source, sink, recv_sem.at[TEMPLATE]).start()
        else:
            deliver(source, sink, TEMPLATE, (to, column), None)
    for i, to in exchange(order):
        deliver(
            target.at[pl.ds(to * planes, planes)],
            target_z.at[:, place, column],
            TARGET,
            (to, owner),
            owner if i == 0 else None,
        )
    before = lax.rem(owner + columns - 1, columns)
    after = lax.rem(owner + 1, columns)

    def act(copy, where, start):
        @pl.when(where == column)
        def _():
            if start:
                pltpu.make_async_copy(copy[0], copy[1], recv_sem.at[copy[2]]).start()

        @pl.when(where != column)
        def _():
            if start:
                remote(*copy).start()
            else:
                remote(*copy).wait_send()

    def act_any(copy, where, i, start):
        if i == 0:
            act(copy, where, start)
        elif start:
            remote(*copy).start()
        else:
            remote(*copy).wait_send()

    def velocity_copies(group, start):
        comps = groups[group]
        for i, to in exchange(order):
            odd = lax.rem(to, 2)
            first = to * planes - 1 + odd

            def piece(low, count, at):
                copy = (
                    velocity.at[comps, pl.ds(low, count)],
                    velocity_z.at[comps, pl.ds(at, count), place, column],
                    VELOCITY + group,
                    (to, owner),
                )
                act_any(copy, owner, i, start)

            @pl.when(jnp.logical_and(to > 0, to < rows - 1))
            def _():
                piece(first, planes + 1, odd)

            @pl.when(to == 0)
            def _():
                piece(0, planes, 1)
                piece(extent_x - 1, 1, 0)

            @pl.when(to == rows - 1)
            def _():
                piece(extent_x - planes, planes, 1)
                piece(0, 1, planes + 1)

    def edge_copies(group, start):
        comps = groups[group]

        def send(line, where):
            for i, to in exchange(order):
                copy = (
                    velocity.at[comps, pl.ds(to * planes, planes)],
                    edge.at[comps, :, line, column],
                    EDGE + group,
                    (to, where),
                )
                act_any(copy, where, i, start)

        @pl.when(place == 0)
        def _():
            send(1, before)

        @pl.when(place == own - 1)
        def _():
            send(0, after)

    velocity_copies(0, True)

    arrived(template_y, TEMPLATE)
    blocks = departure.shape[1]
    span = lines // blocks
    for plane in range(planes):
        image = [template_y[plane, y] for y in range(lines)]
        for block in range(blocks):
            offset = departure[plane, block]
            whole = offset >> (QUANT.bit_length() - 1)
            levels = offset - whole * QUANT
            taps = tap_weights(levels, lambda level, tap: weights[tap, level])
            shift = jnp.where(whole + 1 < 0, whole + 1 + lines, whole + 1)
            rolled = image
            step = 1
            while step < lines:
                chosen = (shift & step) != 0
                rolled = [
                    jnp.where(chosen, rolled[(y - step) % lines], rolled[y]) for y in range(lines)
                ]
                step *= 2
            for y in range(block * span, (block + 1) * span):
                value = taps[0] * rolled[y]
                for tap in range(1, TAPS):
                    value = value + taps[tap] * rolled[(y + tap) % lines]
                extended[plane, y + 1] = value
                if y == lines - 1:
                    extended[plane, 0] = value
                if y == 0:
                    extended[plane, lines + 1] = value
    up, down = lax.rem(row + 1, rows), lax.rem(row + rows - 1, rows)
    for j in range(1, columns):
        to = lax.rem(column + j, columns)
        deliver(
            extended.at[:, pl.ds(to * own, own + 2)],
            moved.at[column],
            MOVED,
            (row, to),
            None,
        )
    for j in range(columns):
        to = lax.rem(column + j, columns)
        lines_of = pl.ds(to * own + 1, own)
        deliver(
            extended.at[planes - 1, lines_of], moved_low.at[:, column], LOW, (up, to), None
        )
        deliver(extended.at[0, lines_of], moved_high.at[:, column], HIGH_SIDE, (down, to), None)
    edge_copies(0, True)
    edge_copies(1, True)
    velocity_copies(1, True)
    moved[column] = extended[:, pl.ds(column * own, own + 2)]
    for load in loads:
        load.wait()

    def whole_lines(values):
        return values.reshape(values.shape[:-3] + (outer, LANES))

    ahead_parts = (ahead[0], ahead[1])
    back_parts = (back[0], back[1])
    def force():
        arrived(target_z, TARGET)
        for _ in range(columns - 1):
            pltpu.make_async_copy(moved.at[0], moved.at[0], recv_sem.at[MOVED]).wait()
        arrived(moved_low, LOW)
        arrived(moved_high, HIGH_SIDE)
        lane = lax.broadcasted_iota(jnp.int32, (own, outer, LANES), 2)
        for plane in range(planes):
            with_ends = jnp.concatenate(
                [moved[j, plane] for j in range(columns)], axis=1
            )
            here = with_ends[1 : own + 1]
            misfit = whole_lines(target_z[plane]) - here
            half = 0.5 * misfit

            def at(index):
                if index < 0:
                    return whole_lines(moved_low[...])
                if index == planes:
                    return whole_lines(moved_high[...])
                return jnp.concatenate(
                    [moved[j, index, 1 : own + 1] for j in range(columns)], axis=1
                )

            rest[0, plane] = half * (at(plane + 1) - at(plane - 1))
            rest[1, plane] = half * (with_ends[2:] - with_ends[:-2])
            following = jnp.roll(here, -1, 2)
            following = jnp.where(lane == LANES - 1, jnp.roll(following, -1, 1), following)
            previous = jnp.roll(here, 1, 2)
            previous = jnp.where(lane == 0, jnp.roll(previous, 1, 1), previous)
            rest[2, plane] = half * (following - previous)

    for group, comps in enumerate(groups):
        if group == len(groups) - 1:
            force()
        arrived(velocity_z.at[comps, pl.ds(parity, planes + 1)], VELOCITY + group)
        arrived(edge.at[comps], EDGE + group)
        deliver(
            velocity_z.at[comps, planes - (planes - 1) * parity],
            velocity_z.at[comps, (planes + 1) * parity],
            SIDE + group,
            (row + 1 - 2 * parity, column),
            None,
        )
        for comp in range(comps.start, comps.start + comps.size):
            for plane in range(planes):
                block = velocity_z[comp, plane + 1].reshape(own * outer, LANES)
                spectrum[:, comp, plane] = dot_split(ahead_parts, split_halves(block)).reshape(
                    outer, own, LANES
                )

    for pair in range(outer // 2):
        shape = (components * planes * own, LANES)
        joined = jnp.concatenate(
            [spectrum[2 * pair].reshape(shape), spectrum[2 * pair + 1].reshape(shape)], axis=1
        )
        result = dot_split(split_halves(joined), (pairs[0, pair], pairs[1, pair]))
        shape = (components, planes, own, LANES)
        spectrum[2 * pair] = result[:, :LANES].reshape(shape)
        spectrum[2 * pair + 1] = result[:, LANES:].reshape(shape)

    for comp in range(components):
        for group, comps in enumerate(groups):
            if comps.start == comp:
                arrived(velocity_z.at[comps, (planes + 1) * (1 - parity)], SIDE + group)
        for plane in range(planes):
            lined = jnp.concatenate(
                [edge[comp, plane, 0:1], velocity_z[comp, plane + 1], edge[comp, plane, 1:2]], axis=0
            )
            sides = (velocity_z[comp, plane] + velocity_z[comp, plane + 2]) + (
                lined[:own] + lined[2:]
            )
            other = rest[comp, plane] - BETA * whole_lines(sides)
            block = jnp.concatenate(
                [
                    spectrum[:, comp, plane].reshape(outer * own, LANES),
                    other.reshape(own * outer, LANES),
                ],
                axis=0,
            )
            result = dot_split(back_parts, split_halves(block))
            for group in range(outer):
                out[comp, plane, :, group * LANES : (group + 1) * LANES] = result[
                    group * own : (group + 1) * own
                ]

    for near, source, sink, kind, to in pending:
        if near is None:
            remote(source, sink, kind, to).wait_send()
        else:

            @pl.when(near != column)
            def _():
                remote(source, sink, kind, to).wait_send()

    for group in range(len(groups)):
        velocity_copies(group, False)
        edge_copies(group, False)


def direct(template, target, velocity, departure, weights):
    rows, columns = lax.axis_size("row"), lax.axis_size("col")
    extent_x, _, cells = template.shape
    components = velocity.shape[0]
    planes = extent_x // rows
    lines = rows
    own = lines // columns
    slab = cells // LANES
    outer = slab * columns
    ahead, pairs, back = operators(cells * columns, own)
    tile = (slab, LANES)
    hbm = pl.BlockSpec(memory_space=pl.ANY)
    vmem = pl.BlockSpec(memory_space=pltpu.VMEM)
    smem = pl.BlockSpec(memory_space=pltpu.SMEM)
    kinds = 5 + 3 * components
    return pl.pallas_call(
        functools.partial(kernel, (rows, columns)),
        out_shape=jax.ShapeDtypeStruct((components, planes, own, outer * LANES), jnp.float32),
        in_specs=[hbm, hbm, hbm, vmem, smem, hbm, hbm, hbm],
        out_specs=vmem,
        scratch_shapes=[
            pltpu.VMEM((planes, lines) + tile, jnp.float32),
            pltpu.VMEM((planes, own, columns) + tile, jnp.float32),
            pltpu.VMEM((components, planes + 2, own, columns) + tile, jnp.float32),
            pltpu.VMEM((components, planes, 2, columns) + tile, jnp.float32),
            pltpu.VMEM((planes, lines + 2) + tile, jnp.float32),
            pltpu.VMEM((columns, planes, own + 2) + tile, jnp.float32),
            pltpu.VMEM((own, columns) + tile, jnp.float32),
            pltpu.VMEM((own, columns) + tile, jnp.float32),
            pltpu.VMEM((components, planes, own, outer, LANES), jnp.float32),
            pltpu.VMEM((outer, components, planes, own, LANES), jnp.float32),
            pltpu.VMEM(ahead.shape, jnp.bfloat16),
            pltpu.VMEM(pairs.shape, jnp.bfloat16),
            pltpu.VMEM(back.shape, jnp.bfloat16),
            pltpu.SemaphoreType.DMA((3,)),
            pltpu.SemaphoreType.DMA((kinds,)),
            pltpu.SemaphoreType.DMA((kinds,)),
        ],
        compiler_params=pltpu.CompilerParams(collective_id=0, has_side_effects=True),
    )(
        template.reshape((extent_x,) + tile),
        target.reshape((extent_x,) + tile),
        velocity.reshape((components, extent_x) + tile),
        departure.reshape(departure.shape[:2] + tile),
        weights.T,
        jnp.asarray(ahead),
        jnp.asarray(pairs),
        jnp.asarray(back),
    )


def per_block(template, target, velocity, departure, weights):
    rows, columns = lax.axis_size("row"), lax.axis_size("col")
    one_line = template.shape[1] == 1 and rows % columns == 0 and rows % 2 == 0 and rows > 2
    whole_tiles = template.shape[2] % (LANES * SUBLANES) == 0
    short = rows // columns % SUBLANES == 0 and rows >= 8
    if one_line and whole_tiles and short:
        return direct(template, target, velocity, departure, weights)
    return per_device(template, target, velocity, departure, weights)


def solution(mesh):
    in_specs = (
        P(None, "row", "col"),
        P(None, "row", "col"),
        P(None, None, "row", "col"),
        P("row", None, "col"),
        P(),
    )
    out_specs = P(None, "row", "col", None)
    return jax.shard_map(
        per_block, mesh=mesh, in_specs=in_specs, out_specs=out_specs, check_vma=False
    )
```

```python
import functools
import math

import jax
import jax.numpy as jnp
import numpy as np
from jax import lax
from jax.experimental import pallas as pl
from jax.experimental.pallas import tpu as pltpu
from jax.sharding import PartitionSpec as P

QUANT = 8
TAPS = 4


BETA = 0.5
HIGH = lax.Precision.HIGHEST
LANES = 128
SUBLANES = 8
MESH = pl.DeviceIdType.MESH


def with_halo(block, sides, width):
    for axis, dim in sides:
        count = lax.axis_size(axis)
        forward = [(i, i + 1) for i in range(count - 1)]
        forward.append((count - 1, 0))
        backward = [(target, source) for source, target in forward]
        low = lax.ppermute(
            lax.slice_in_dim(block, block.shape[dim] - width, None, axis=dim), axis, forward
        )
        high = lax.ppermute(lax.slice_in_dim(block, 0, width, axis=dim), axis, backward)
        block = jnp.concatenate([low, block, high], axis=dim)
    return block


def central(values, axis):
    return (jnp.roll(values, -1, axis) - jnp.roll(values, 1, axis)) * 0.5


def second_difference(values, axis):
    return 2.0 * values - jnp.roll(values, -1, axis) - jnp.roll(values, 1, axis)


def tap_weights(levels, weight):
    taps = []
    for tap in range(TAPS):
        value = jnp.zeros(levels.shape, jnp.float32)
        for level in range(QUANT):
            value = jnp.where(levels == level, weight(level, tap), value)
        taps.append(value)
    return taps


def transport(template_y, departure, weights):
    planes, lines, columns = template_y.shape
    blocks = departure.shape[1]
    span = lines // blocks
    shift_cells = jnp.floor_divide(departure, QUANT)
    levels = departure - shift_cells * QUANT
    taps = tap_weights(levels, lambda level, tap: weights[level, tap])
    shift = jnp.mod(shift_cells + 1, lines)
    parts = []
    for block in range(blocks):
        rolled = template_y
        step = 1
        while step < lines:
            chosen = (shift[:, block : block + 1] & step) != 0
            rolled = jnp.where(chosen, jnp.roll(rolled, step, 1), rolled)
            step *= 2
        part = 0.0
        for tap in range(TAPS):
            turned = jnp.roll(rolled, -tap - block * span, 1)[:, :span]
            part = part + taps[tap][:, block : block + 1] * turned
        parts.append(part)
    return jnp.concatenate(parts, axis=1)


def curvature(velocity_z):
    field_shape = velocity_z.shape
    length = field_shape[-1]
    inner = 128
    outer = length // inner
    lines = velocity_z.reshape(-1, outer, inner)
    angle = 2.0 * math.pi / length
    outer_index = jnp.arange(outer, dtype=jnp.int32)
    inner_index = jnp.arange(inner, dtype=jnp.int32)
    outer_phase = (
        jnp.mod(outer_index[:, None] * outer_index[None, :] * inner, length).astype(jnp.float32)
        * angle
    )
    cos_outer = jnp.cos(outer_phase)
    sin_outer = jnp.sin(outer_phase)
    twist_phase = (
        jnp.mod(outer_index[:, None] * inner_index[None, :], length).astype(jnp.float32) * angle
    )
    cos_twist = jnp.cos(twist_phase)
    sin_twist = jnp.sin(twist_phase)
    inner_phase = (
        jnp.mod(inner_index[:, None] * inner_index[None, :] * outer, length).astype(jnp.float32)
        * angle
    )
    cos_inner = jnp.cos(inner_phase)
    sin_inner = jnp.sin(inner_phase)
    freq_index = outer_index[:, None] + outer * inner_index[None, :]
    signed = jnp.where(freq_index < length // 2, freq_index, freq_index - length).astype(
        jnp.float32
    )
    symbol = (signed * angle) ** 2 / length
    real_one = jnp.einsum("lap,ak->lkp", lines, cos_outer, precision=HIGH)
    imag_one = -jnp.einsum("lap,ak->lkp", lines, sin_outer, precision=HIGH)
    real_two = real_one * cos_twist + imag_one * sin_twist
    imag_two = imag_one * cos_twist - real_one * sin_twist
    real_three = jnp.einsum("lkp,pq->lkq", real_two, cos_inner, precision=HIGH) + jnp.einsum(
        "lkp,pq->lkq", imag_two, sin_inner, precision=HIGH
    )
    imag_three = jnp.einsum("lkp,pq->lkq", imag_two, cos_inner, precision=HIGH) - jnp.einsum(
        "lkp,pq->lkq", real_two, sin_inner, precision=HIGH
    )
    real_three = real_three * symbol
    imag_three = imag_three * symbol
    real_four = jnp.einsum("lkq,pq->lkp", real_three, cos_inner, precision=HIGH) - jnp.einsum(
        "lkq,pq->lkp", imag_three, sin_inner, precision=HIGH
    )
    imag_four = jnp.einsum("lkq,pq->lkp", imag_three, cos_inner, precision=HIGH) + jnp.einsum(
        "lkq,pq->lkp", real_three, sin_inner, precision=HIGH
    )
    real_five = real_four * cos_twist - imag_four * sin_twist
    imag_five = imag_four * cos_twist + real_four * sin_twist
    result = jnp.einsum("lkp,kn->lnp", real_five, cos_outer, precision=HIGH) - jnp.einsum(
        "lkp,kn->lnp", imag_five, sin_outer, precision=HIGH
    )
    return result.reshape(field_shape)


def spectral(arrived):
    return (arrived, curvature(arrived[3:6]))


def per_device(template, target, velocity, departure, weights):
    across = second_difference(velocity, 1)
    bundle = jnp.concatenate([template[None], target[None], velocity, across], axis=0)
    regrouped = lax.all_to_all(bundle, "row", split_axis=1, concat_axis=2, tiled=True)
    moved_image = transport(regrouped[0], departure, weights)
    misfit = regrouped[1] - moved_image
    pull_along = misfit * central(moved_image, 1)
    velocity_y = regrouped[2:5]
    second_part = second_difference(velocity_y, 2)
    second_part = regrouped[5:8] + second_part
    outgoing = jnp.concatenate(
        [misfit[None], moved_image[None], pull_along[None], velocity_y, second_part], axis=0
    )
    columns_z, bending = spectral(
        lax.all_to_all(outgoing, "col", split_axis=2, concat_axis=3, tiled=True)
    )
    misfit_z = columns_z[0]
    moved_z = columns_z[1]
    second_z = columns_z[6:9]
    padded = with_halo(moved_z, (("row", 0),), 1)
    slope_across = (padded[2:] - padded[:-2]) * 0.5
    force = jnp.stack([misfit_z * slope_across, columns_z[2], misfit_z * central(moved_z, 2)])
    return BETA * (second_z + bending) + force


QUAD = 4


def split_halves(values):
    high = values.astype(jnp.bfloat16)
    return high, (values - high.astype(jnp.float32)).astype(jnp.bfloat16)


def dot_split(left, right):
    dot = functools.partial(jnp.dot, preferred_element_type=jnp.float32)
    return dot(left[0], right[0]) + (dot(left[0], right[1]) + dot(left[1], right[0]))


def halves_of(matrix):
    high = matrix.astype(np.float32).astype(jnp.bfloat16)
    low = (matrix - high.astype(np.float64)).astype(np.float32).astype(jnp.bfloat16)
    return np.stack([high, low])


def operators(length, rows):
    outer = length // LANES
    frequency = np.fft.fftfreq(length) * length
    response = np.real(np.fft.ifft((2.0 * math.pi / length * frequency) ** 2))
    response[0] += 4.0
    response *= BETA
    inner = np.arange(LANES)
    group = np.arange(outer)
    away = np.mod(
        LANES * group[:, None, None] + inner[None, :, None] - inner[None, None, :], length
    )
    mixed = np.fft.fft(response[away], axis=0)
    pairs = []
    forward = np.zeros((outer, outer))
    inverse = np.zeros((outer, outer))
    forward[0] = 1.0
    forward[1] = (-1.0) ** group
    inverse[:, 0] = 1.0 / outer
    inverse[:, 1] = (-1.0) ** group / outer
    zero = np.zeros((LANES, LANES))
    pairs.append(np.block([[mixed[0].real.T, zero], [zero, mixed[outer // 2].real.T]]))
    for k in range(1, outer // 2):
        real, imag = mixed[k].real.T, mixed[k].imag.T
        pairs.append(np.block([[real, imag], [-imag, real]]))
        phase = 2.0 * math.pi * k * group / outer
        forward[2 * k] = np.cos(phase)
        forward[2 * k + 1] = -np.sin(phase)
        inverse[:, 2 * k] = 2.0 * np.cos(phase) / outer
        inverse[:, 2 * k + 1] = -2.0 * np.sin(phase) / outer
    same = np.eye(rows)
    ahead = np.einsum("ka,yz->kyza", forward, same).reshape(outer * rows, rows * outer)
    back = np.einsum("ak,yz->aykz", inverse, same).reshape(outer * rows, outer * rows)
    moves = np.einsum("ab,yz->ayzb", np.eye(outer), same).reshape(outer * rows, rows * outer)
    back = np.concatenate([back, moves], axis=1)
    return halves_of(ahead), halves_of(np.stack(pairs)), halves_of(back)


def kernel(
    extent,
    template,
    target,
    velocity,
    departure,
    weights,
    ahead_hbm,
    pairs_hbm,
    back_hbm,
    out,
    template_y,
    target_z,
    velocity_z,
    edge,
    extended,
    moved,
    moved_low,
    moved_high,
    rest,
    spectrum,
    ahead,
    pairs,
    back,
    load_sem,
    send_sem,
    recv_sem,
):
    rows, columns = extent
    row, column = lax.axis_index("row"), lax.axis_index("col")
    planes, lines, slab = template_y.shape[:3]
    components = velocity_z.shape[0]
    own = lines // columns
    outer = columns * slab
    owner = row // own
    place = lax.rem(row, own)
    TEMPLATE, TARGET, MOVED, LOW, HIGH_SIDE, VELOCITY = 0, 1, 2, 3, 4, 5
    SIDE_LOW, SIDE_HIGH, EDGE_LOW, EDGE_HIGH = (VELOCITY + i * components for i in range(1, 5))
    extent_x = velocity.shape[1]
    spot = lax.rem(row, QUAD)
    groups = [pl.ds(0, components - 1), pl.ds(components - 1, 1)]

    loads = [
        pltpu.make_async_copy(source, sink, load_sem.at[i])
        for i, (source, sink) in enumerate(
            [(ahead_hbm, ahead), (pairs_hbm, pairs), (back_hbm, back)]
        )
    ]
    for load in loads:
        load.start()

    barrier = pltpu.get_barrier_semaphore()
    for i in range(rows):
        for j in range(columns):
            if i + j > 0:
                pl.semaphore_signal(
                    barrier,
                    inc=1,
                    device_id=(lax.rem(row + i, rows), lax.rem(column + j, columns)),
                    device_id_type=MESH,
                )
    pl.semaphore_wait(barrier, rows * columns - 1)

    def remote(source, sink, kind, to):
        return pltpu.make_async_remote_copy(
            src_ref=source,
            dst_ref=sink,
            send_sem=send_sem.at[kind],
            recv_sem=recv_sem.at[kind],
            device_id=to,
            device_id_type=MESH,
        )

    pending = []

    def deliver(source, sink, kind, to, near):
        if near is None:
            remote(source, sink, kind, to).start()
            pending.append((None, source, sink, kind, to))
            return

        @pl.when(near == column)
        def _():
            pltpu.make_async_copy(source, sink, recv_sem.at[kind]).start()

        @pl.when(near != column)
        def _():
            remote(source, sink, kind, to).start()

        pending.append((near, source, sink, kind, to))

    def exchange(order):
        return [(i, lax.rem(row + i, rows)) for i in order]

    def arrived(ref, kind):
        pltpu.make_async_copy(ref, ref, recv_sem.at[kind]).wait()

    order = sorted(range(rows), key=lambda i: abs(2 * i - rows))
    for i, to in exchange(order):
        source = template.at[pl.ds(to * planes, planes)]
        sink = template_y.at[:, row]
        if i == 0:
            pltpu.make_async_copy(source, sink, recv_sem.at[TEMPLATE]).start()
        else:
            deliver(source, sink, TEMPLATE, (to, column), None)
    for i, to in exchange(order):
        deliver(
            target.at[pl.ds(to * planes, planes)],
            target_z.at[:, place, column],
            TARGET,
            (to, owner),
            owner if i == 0 else None,
        )
    before = lax.rem(owner + columns - 1, columns)
    after = lax.rem(owner + 1, columns)

    def away_start(*copy):
        remote(*copy).start()

    def away_wait(*copy):
        remote(*copy).wait_send()

    def inside(source, sink, kind, _):
        pltpu.make_async_copy(source, sink, recv_sem.at[kind]).start()

    def velocity_copies(group, start):
        comps = groups[group]
        for i, to in exchange(order):
            at_spot = lax.rem(to, QUAD)
            first = to * planes
            case = jnp.where(at_spot == 0, 0, jnp.where(at_spot == QUAD - 1, 2, 1))
            case = jnp.where(to == 0, 3, jnp.where(to == rows - 1, 4, case))

            def pieces(case, act):
                def piece(low, count, at):
                    act(
                        velocity.at[comps, pl.ds(low, count)],
                        velocity_z.at[comps, pl.ds(at, count), place, column],
                        VELOCITY + group,
                        (to, owner),
                    )

                @pl.when(case == 1)
                def _():
                    piece(first, planes, 1)

                @pl.when(case == 0)
                def _():
                    piece(first - 1, planes + 1, 0)

                @pl.when(case == 2)
                def _():
                    piece(first, planes + 1, 1)

                @pl.when(case == 3)
                def _():
                    piece(0, planes, 1)
                    piece(extent_x - 1, 1, 0)

                @pl.when(case == 4)
                def _():
                    piece(extent_x - planes, planes, 1)
                    piece(0, 1, planes + 1)

            away = away_start if start else away_wait
            if i > 0:
                pieces(case, away)
                continue
            pieces(jnp.where(owner == column, -1, case), away)
            if start:
                pieces(jnp.where(owner == column, case, -1), inside)

    def beside(group, start):
        comps = groups[group]
        mine = pl.ds(1, planes)

        def go(*copy):
            if start:
                remote(*copy).start()
            else:
                remote(*copy).wait_send()

        go(
            velocity_z.at[comps, mine, own - 1],
            edge.at[comps, :, 0],
            EDGE_LOW + group,
            (row, lax.rem(column + 1, columns)),
        )
        go(
            velocity_z.at[comps, mine, 0],
            edge.at[comps, :, 1],
            EDGE_HIGH + group,
            (row, lax.rem(column + columns - 1, columns)),
        )

        @pl.when(spot < QUAD - 1)
        def _():
            go(
                velocity_z.at[comps, planes],
                velocity_z.at[comps, 0],
                SIDE_LOW + group,
                (lax.rem(row + 1, rows), column),
            )

        @pl.when(spot > 0)
        def _():
            go(
                velocity_z.at[comps, 1],
                velocity_z.at[comps, planes + 1],
                SIDE_HIGH + group,
                (lax.rem(row + rows - 1, rows), column),
            )

    velocity_copies(0, True)

    arrived(template_y, TEMPLATE)
    blocks = departure.shape[1]
    span = lines // blocks
    for plane in range(planes):
        image = [template_y[plane, y] for y in range(lines)]
        for block in range(blocks):
            offset = departure[plane, block]
            whole = offset >> (QUANT.bit_length() - 1)
            levels = offset - whole * QUANT
            taps = tap_weights(levels, lambda level, tap: weights[tap, level])
            shift = jnp.where(whole + 1 < 0, whole + 1 + lines, whole + 1)
            rolled = image
            step = 1
            while step < lines:
                chosen = (shift & step) != 0
                rolled = [
                    jnp.where(chosen, rolled[(y - step) % lines], rolled[y]) for y in range(lines)
                ]
                step *= 2
            for y in range(block * span, (block + 1) * span):
                value = taps[0] * rolled[y]
                for tap in range(1, TAPS):
                    value = value + taps[tap] * rolled[(y + tap) % lines]
                extended[plane, y + 1] = value
                if y == lines - 1:
                    extended[plane, 0] = value
                if y == 0:
                    extended[plane, lines + 1] = value
    up, down = lax.rem(row + 1, rows), lax.rem(row + rows - 1, rows)
    for j in range(1, columns):
        to = lax.rem(column + j, columns)
        deliver(
            extended.at[:, pl.ds(to * own, own + 2)],
            moved.at[column],
            MOVED,
            (row, to),
            None,
        )
    for j in range(columns):
        to = lax.rem(column + j, columns)
        lines_of = pl.ds(to * own + 1, own)
        deliver(
            extended.at[planes - 1, lines_of], moved_low.at[:, column], LOW, (up, to), None
        )
        deliver(extended.at[0, lines_of], moved_high.at[:, column], HIGH_SIDE, (down, to), None)
    velocity_copies(1, True)
    moved[column] = extended[:, pl.ds(column * own, own + 2)]
    for load in loads:
        load.wait()

    def whole_lines(values):
        return values.reshape(values.shape[:-3] + (outer, LANES))

    ahead_parts = (ahead[0], ahead[1])
    back_parts = (back[0], back[1])
    def force():
        arrived(target_z, TARGET)
        for _ in range(columns - 1):
            pltpu.make_async_copy(moved.at[0], moved.at[0], recv_sem.at[MOVED]).wait()
        arrived(moved_low, LOW)
        arrived(moved_high, HIGH_SIDE)
        lane = lax.broadcasted_iota(jnp.int32, (own, outer, LANES), 2)
        for plane in range(planes):
            with_ends = jnp.concatenate(
                [moved[j, plane] for j in range(columns)], axis=1
            )
            here = with_ends[1 : own + 1]
            misfit = whole_lines(target_z[plane]) - here
            half = 0.5 * misfit

            def at(index):
                if index < 0:
                    return whole_lines(moved_low[...])
                if index == planes:
                    return whole_lines(moved_high[...])
                return jnp.concatenate(
                    [moved[j, index, 1 : own + 1] for j in range(columns)], axis=1
                )

            rest[0, plane] = half * (at(plane + 1) - at(plane - 1))
            rest[1, plane] = half * (with_ends[2:] - with_ends[:-2])
            following = jnp.roll(here, -1, 2)
            following = jnp.where(lane == LANES - 1, jnp.roll(following, -1, 1), following)
            previous = jnp.roll(here, 1, 2)
            previous = jnp.where(lane == 0, jnp.roll(previous, 1, 1), previous)
            rest[2, plane] = half * (following - previous)

    for group, comps in enumerate(groups):
        if group == len(groups) - 1:
            force()

        @pl.when(spot == 0)
        def _():
            arrived(velocity_z.at[comps, pl.ds(0, planes + 1)], VELOCITY + group)

        @pl.when(spot == QUAD - 1)
        def _():
            arrived(velocity_z.at[comps, pl.ds(1, planes + 1)], VELOCITY + group)

        @pl.when(spot * (QUAD - 1 - spot) > 0)
        def _():
            arrived(velocity_z.at[comps, pl.ds(1, planes)], VELOCITY + group)

        beside(group, True)
        for comp in range(comps.start, comps.start + comps.size):
            for plane in range(planes):
                block = velocity_z[comp, plane + 1].reshape(own * outer, LANES)
                spectrum[:, comp, plane] = dot_split(ahead_parts, split_halves(block)).reshape(
                    outer, own, LANES
                )

    for pair in range(outer // 2):
        shape = (components * planes * own, LANES)
        joined = jnp.concatenate(
            [spectrum[2 * pair].reshape(shape), spectrum[2 * pair + 1].reshape(shape)], axis=1
        )
        result = dot_split(split_halves(joined), (pairs[0, pair], pairs[1, pair]))
        shape = (components, planes, own, LANES)
        spectrum[2 * pair] = result[:, :LANES].reshape(shape)
        spectrum[2 * pair + 1] = result[:, LANES:].reshape(shape)

    for comp in range(components):
        for group, comps in enumerate(groups):
            if comps.start == comp:
                arrived(edge.at[comps, :, 0], EDGE_LOW + group)
                arrived(edge.at[comps, :, 1], EDGE_HIGH + group)

                @pl.when(spot > 0)
                def _():
                    arrived(velocity_z.at[comps, 0], SIDE_LOW + group)

                @pl.when(spot < QUAD - 1)
                def _():
                    arrived(velocity_z.at[comps, planes + 1], SIDE_HIGH + group)

        for plane in range(planes):
            lined = jnp.concatenate(
                [edge[comp, plane, 0:1], velocity_z[comp, plane + 1], edge[comp, plane, 1:2]], axis=0
            )
            sides = (velocity_z[comp, plane] + velocity_z[comp, plane + 2]) + (
                lined[:own] + lined[2:]
            )
            other = rest[comp, plane] - BETA * whole_lines(sides)
            block = jnp.concatenate(
                [
                    spectrum[:, comp, plane].reshape(outer * own, LANES),
                    other.reshape(own * outer, LANES),
                ],
                axis=0,
            )
            result = dot_split(back_parts, split_halves(block))
            for group in range(outer):
                out[comp, plane, :, group * LANES : (group + 1) * LANES] = result[
                    group * own : (group + 1) * own
                ]

    for near, source, sink, kind, to in pending:
        if near is None:
            remote(source, sink, kind, to).wait_send()
        else:

            @pl.when(near != column)
            def _():
                remote(source, sink, kind, to).wait_send()

    for group in range(len(groups)):
        velocity_copies(group, False)
        beside(group, False)


def direct(template, target, velocity, departure, weights):
    rows, columns = lax.axis_size("row"), lax.axis_size("col")
    extent_x, _, cells = template.shape
    components = velocity.shape[0]
    planes = extent_x // rows
    lines = rows
    own = lines // columns
    slab = cells // LANES
    outer = slab * columns
    ahead, pairs, back = operators(cells * columns, own)
    tile = (slab, LANES)
    hbm = pl.BlockSpec(memory_space=pl.ANY)
    vmem = pl.BlockSpec(memory_space=pltpu.VMEM)
    smem = pl.BlockSpec(memory_space=pltpu.SMEM)
    kinds = 5 + 5 * components
    return pl.pallas_call(
        functools.partial(kernel, (rows, columns)),
        out_shape=pltpu.VMEM((components, planes, own, outer * LANES), jnp.float32),
        in_specs=[hbm, hbm, hbm, vmem, smem, hbm, hbm, hbm],
        out_specs=vmem,
        scratch_shapes=[
            pltpu.VMEM((planes, lines) + tile, jnp.float32),
            pltpu.VMEM((planes, own, columns) + tile, jnp.float32),
            pltpu.VMEM((components, planes + 2, own, columns) + tile, jnp.float32),
            pltpu.VMEM((components, planes, 2, columns) + tile, jnp.float32),
            pltpu.VMEM((planes, lines + 2) + tile, jnp.float32),
            pltpu.VMEM((columns, planes, own + 2) + tile, jnp.float32),
            pltpu.VMEM((own, columns) + tile, jnp.float32),
            pltpu.VMEM((own, columns) + tile, jnp.float32),
            pltpu.VMEM((components, planes, own, outer, LANES), jnp.float32),
            pltpu.VMEM((outer, components, planes, own, LANES), jnp.float32),
            pltpu.VMEM(ahead.shape, jnp.bfloat16),
            pltpu.VMEM(pairs.shape, jnp.bfloat16),
            pltpu.VMEM(back.shape, jnp.bfloat16),
            pltpu.SemaphoreType.DMA((3,)),
            pltpu.SemaphoreType.DMA((kinds,)),
            pltpu.SemaphoreType.DMA((kinds,)),
        ],
        compiler_params=pltpu.CompilerParams(collective_id=0, has_side_effects=True),
    )(
        template.reshape((extent_x,) + tile),
        target.reshape((extent_x,) + tile),
        velocity.reshape((components, extent_x) + tile),
        departure.reshape(departure.shape[:2] + tile),
        weights.T,
        jnp.asarray(ahead),
        jnp.asarray(pairs),
        jnp.asarray(back),
    )


def per_block(template, target, velocity, departure, weights):
    rows, columns = lax.axis_size("row"), lax.axis_size("col")
    components = velocity.shape[0]
    one_line = template.shape[1] == 1 and rows % columns == 0 and rows % QUAD == 0 and columns > 1 and components > 1
    whole_tiles = template.shape[2] % (LANES * SUBLANES) == 0
    short = rows // columns % SUBLANES == 0 and rows >= 8
    if one_line and whole_tiles and short:
        return direct(template, target, velocity, departure, weights)
    return per_device(template, target, velocity, departure, weights)


def solution(mesh):
    in_specs = (
        P(None, "row", "col"),
        P(None, "row", "col"),
        P(None, None, "row", "col"),
        P("row", None, "col"),
        P(),
    )
    out_specs = P(None, "row", "col", None)
    return jax.shard_map(
        per_block, mesh=mesh, in_specs=in_specs, out_specs=out_specs, check_vma=False
    )
```
